512 devices in a mesh: row: 16 (over x_hi, z), col: 32 (over y, x_lo, core).
Axes of the slice: x: 4 (x_hi: 2, x_lo: 2; x = x_hi * 2 + x_lo), y: 8, z: 8, core: 2. Of those that a mesh axis runs over, the one named last changes fastest.
Arguments:
- activations: bfloat16 [1024, 28672], P('row', 'col'), may hold values from -0.1875 to 0.1875
- cotangent: bfloat16 [1024, 16384], P('col', 'row'), may hold values from -6 to 6
- down_weight: bfloat16 [28672, 16384], P('col', 'row'), may hold values from -0.046875 to 0.046875
- row_order: int32 [1024], replicated, may hold values from 0 to 1023, each once
Outputs:
- weight_grad: bfloat16 [28672, 16384], P('col', 'row')
- input_grad: bfloat16 [1024, 28672], P('row', 'col')
The draws below stay inside these ranges and needn't reach their ends.
Inputs may be any that keep to these rules, and one draw needn't show every extreme that they name: `row_order`: each of the 1024 rows is named exactly once.
All inputs are finite; a program needn't handle non-finite values.
Results may differ from the reference program's by a relative error of at most 0.001.
Values may be sent and summed in bfloat16 or wider, within the bound.
A program may use at most 64 MiB of HBM per device.

```python
import jax
import jax.numpy as jnp

D = 16384
F = 28672
ROWS = 1024


def with_spikes(result, stream_key, source, target, blocks, factor):
    def block_of(position):
        return (jnp.arange(result.shape[position]) // (result.shape[position] // blocks)).reshape((-1,) + (1,) * (result.ndim - 1 - position))

    first = jax.random.permutation(stream_key, blocks)[block_of(target)]
    far = (block_of(target) + blocks // 2) % blocks
    return jnp.where((block_of(source) == first) | (block_of(source) == far), factor * result, result)


def shard_levels(own_key, dims, pieces, least, top_value):
    def one(axis_at, blocks):
        heights = jax.random.uniform(jax.random.fold_in(jax.random.fold_in(own_key, 6), axis_at), (blocks,), jnp.float32, least / len(pieces), top_value / len(pieces))
        return jnp.repeat(jnp.exp(heights), dims[axis_at] // blocks).reshape((-1,) + (1,) * (len(dims) - axis_at - 1))

    gain = one(*pieces[0])
    for cut in pieces[1:]:
        gain = gain * one(*cut)
    return gain


def gaussian(rng, dims, deviation, most, pieces=(), dtype=jnp.bfloat16):
    drawn = jax.random.normal(rng, dims, jnp.float32) * deviation
    if len(pieces) > 0:
        drawn = shard_levels(rng, dims, pieces, -0.22, 0.18) * drawn
    return jnp.clip(drawn, min=-most, max=most).astype(dtype)


def gaussian_with(own_key, shape, spread, most, shards, heavy, kind=jnp.bfloat16):
    entries = spread * jax.random.normal(own_key, shape, jnp.float32)
    if shards:
        entries = entries * shard_levels(own_key, shape, shards, -0.22, 0.18)
    return jnp.clip(with_spikes(entries, jax.random.fold_in(own_key, 3), *heavy), -most, most).astype(kind)


def setup_inputs(seed: int = 0) -> dict:
    seeds = jax.random.split(jax.random.key(seed), 5)
    activations = gaussian(seeds[0], (ROWS, F), (1.0 / ROWS ** 0.5), 0.1875, ((0, 16), (1, 32)))
    cotangent = gaussian_with(seeds[1], (ROWS, D), 1.0, 6.0, ((0, 32), (1, 16)), (1, 0, 32, 2.75))
    down_weight = gaussian(seeds[2], (F, D), D ** -0.5, 0.046875, ((0, 32), (1, 16)))
    row_order = jax.random.permutation(seeds[3], ROWS).astype(jnp.int32)
    return {"activations": activations, "cotangent": cotangent, "down_weight": down_weight, "row_order": row_order}


def reference(activations, cotangent, down_weight, row_order):
    aligned = jnp.take(cotangent, row_order.astype(jnp.int32), axis=0)
    weight_grad = jnp.dot(activations.T, aligned, preferred_element_type=jnp.float32).astype(jnp.bfloat16)
    input_grad = jnp.dot(aligned, down_weight.T, preferred_element_type=jnp.float32).astype(jnp.bfloat16)
    return weight_grad, input_grad
```

```python
import functools

import jax
import jax.numpy as jnp
from jax import lax
from jax.experimental import pallas as pl
from jax.experimental.pallas import tpu as pltpu
from jax.sharding import PartitionSpec as P

MESH = pl.DeviceIdType.MESH
RING = 8
FAR = RING // 2
GROUPS = [(FAR, 0), (FAR, 1)]
for _d in (3, 2, 1):
    GROUPS += [(_d, 0), (_d, 1), (-_d, 0), (-_d, 1)]
GROUPS += [(0, 0), (0, 1)]
PLACE = {g: i for i, g in enumerate(GROUPS)}
F32 = jnp.float32
BF16 = jnp.bfloat16


def z_place(distance, half):
    if distance in (FAR, -FAR):
        distance = FAR
    return PLACE[(distance, half)]


def hops(direction, stream):
    return FAR if (direction == 1) == (stream == 0) else FAR - 1


STREAMS = [(d, s) for s in (0, 1) for d in (1, -1)]


def dot_nt(a, b):
    return lax.dot_general(a, b, (((1,), (1,)), ((), ())), preferred_element_type=F32)


def dot_tn(a, b):
    return lax.dot_general(a, b, (((0,), (0,)), ((), ())), preferred_element_type=F32)


def kernel(
    act, cot, weight, order, wgrad, igrad,
    cot_all, act_all, w_vmem, place_col, pick, aligned, partial,
    out_val, out_scale, in_val, in_scale,
    g_send, g_recv, s_send, s_recv, a_send, a_recv, r_send, r_recv, c_send, c_recv, local_sem,
):
    row, col = lax.axis_index("row"), lax.axis_index("col")
    xh, z = row // RING, lax.rem(row, RING)
    y, xl, core = col // 4, lax.rem(col, 4) // 2, lax.rem(col, 2)

    def at_z(step):
        return (xh * RING + lax.rem(z + step + RING, RING), col)

    def at_y(step):
        return (row, lax.rem(y + step + RING, RING) * 4 + xl * 2 + core)

    x_far = ((1 - xh) * RING + z, col)
    x_near = (row, y * 4 + (1 - xl) * 2 + core)
    sibling = (row, y * 4 + xl * 2 + 1 - core)

    rows_g = cot.shape[0]
    rows_a, hidden = act.shape
    total = cot_all.shape[0]
    half = total // 2

    def g_slot(core_d, y_d, x_d):
        return cot_all.at[pl.ds(core_d * half + ((y_d % RING) * 2 + x_d) * rows_g, rows_g)]

    def a_rows(distance, h):
        return pl.ds(z_place(distance, h) * rows_a, rows_a)

    def remote(src, dst, send, recv, device):
        return pltpu.make_async_remote_copy(
            src_ref=src, dst_ref=dst, send_sem=send, recv_sem=recv, device_id=device, device_id_type=MESH
        )

    barrier = pltpu.get_barrier_semaphore()
    partners = (at_y(1), at_y(-1), x_near, sibling, at_z(1), at_z(-1), x_far)
    for device in partners:
        pl.semaphore_signal(barrier, inc=1, device_id=device, device_id_type=MESH)
    pl.semaphore_wait(barrier, len(partners))

    sent = []

    def start(copy):
        copy.start()
        sent.append(copy)
        return copy

    g_ring = {}
    n = 0
    for step in range(1, FAR + 1):
        for d, s in STREAMS:
            if step <= hops(d, s):
                src = cot if (step == 1 and s == 0) else g_slot(0, -d * (step - 1), s)
                g_ring[(step, d, s)] = remote(src, g_slot(0, -d * step, s), g_send.at[n], g_recv.at[n], at_y(d))
                n += 1
    g_near = remote(cot, g_slot(0, 0, 1), g_send.at[n], g_recv.at[n], x_near)
    s_copies = {}
    for y_d in range(RING):
        for x_d in range(2):
            i = y_d * 2 + x_d
            src = cot if i == 0 else g_slot(0, y_d, x_d)
            s_copies[(y_d, x_d)] = remote(src, g_slot(1, y_d, x_d), s_send.at[i], s_recv.at[i], sibling)

    a_ring = {}
    n = 0
    for step in range(1, FAR + 1):
        for d, s in STREAMS:
            if step <= hops(d, s):
                src = act if (step == 1 and s == 0) else act_all.at[a_rows(-d * (step - 1), s)]
                a_ring[(step, d, s)] = remote(src, act_all.at[a_rows(-d * step, s)], a_send.at[n], a_recv.at[n], at_z(d))
                n += 1
    a_far = remote(act, act_all.at[a_rows(0, 1)], a_send.at[n], a_recv.at[n], x_far)

    start(g_near)
    start(g_ring[(1, 1, 0)])
    start(g_ring[(1, -1, 0)])
    start(a_far)
    start(a_ring[(1, 1, 0)])
    start(a_ring[(1, -1, 0)])
    start(s_copies[(0, 0)])
    own_g = pltpu.make_async_copy(cot, g_slot(0, 0, 0), local_sem.at[0])
    own_a = pltpu.make_async_copy(act, act_all.at[a_rows(0, 0)], local_sem.at[1])
    own_w = pltpu.make_async_copy(weight, w_vmem, local_sem.at[2])
    own_g.start()
    own_a.start()
    own_w.start()

    r = order[...]
    spot = (
        lax.rem(r // 32 + core, 2) * half
        + lax.rem(r // 128 - y + RING, RING) * (2 * rows_g)
        + lax.rem(r // 64 + xl, 2) * rows_g
        + lax.rem(r, 32)
    ).astype(F32)
    for b in range(total // 128):
        place_col[b * 128:(b + 1) * 128, :] = jnp.transpose(jnp.broadcast_to(spot[b:b + 1, :], (128, 128)))

    g_near.wait_recv()
    start(g_ring[(1, 1, 1)])
    start(g_ring[(1, -1, 1)])
    start(s_copies[(0, 1)])
    a_far.wait_recv()
    start(a_ring[(1, 1, 1)])
    start(a_ring[(1, -1, 1)])

    lanes = lax.broadcasted_iota(jnp.int32, (rows_a, 128), 1).astype(F32)

    def build_pick(first, last):
        for i in range(first, last):
            distance, h = GROUPS[i]
            shard = lax.rem(xh + h, 2) * RING + lax.rem(z + distance + RING, RING)
            want = place_col[pl.ds(pl.multiple_of(shard * rows_a, rows_a), rows_a), :]
            for j in range(total // 128):
                hit = jnp.where(want == lanes + float(j * 128), 1.0, 0.0).astype(F32)
                pick[i * rows_a:(i + 1) * rows_a, j * 128:(j + 1) * 128] = hit.astype(BF16)

    def g_step(step):
        for d, s in STREAMS:
            if step <= hops(d, s):
                g_ring[(step, d, s)].wait_recv()
                if step < hops(d, s):
                    start(g_ring[(step + 1, d, s)])
                start(s_copies[((-d * step) % RING, s)])

    def a_step(step):
        for d, s in STREAMS:
            if step <= hops(d, s):
                a_ring[(step, d, s)].wait_recv()
                if step < hops(d, s):
                    start(a_ring[(step + 1, d, s)])

    build_pick(0, 6)
    g_step(1)
    build_pick(6, 11)
    g_step(2)
    a_step(1)
    build_pick(11, 16)
    g_step(3)
    a_step(2)
    g_step(4)
    own_g.wait()
    for key in s_copies:
        s_copies[key].wait_recv()
    own_w.wait()

    def sums(first, last):
        rows = slice(first * rows_a, last * rows_a)
        aligned[rows, :] = jnp.dot(pick[rows, :], cot_all[...], preferred_element_type=F32).astype(BF16)
        partial[rows, :] = dot_nt(aligned[rows, :], w_vmem[...])

    def part_of(distance, h):
        i = z_place(distance, h)
        return partial[i * rows_a:(i + 1) * rows_a, :]

    def encode(value, slot):
        top = jnp.maximum(jnp.max(jnp.abs(value), axis=0, keepdims=True), 1e-34)
        out_val[slot] = jnp.round(value * (32767.0 / top)).astype(jnp.int32).astype(jnp.int16)
        out_scale[slot] = top * (1.0 / 32767.0)

    def decode(slot):
        return in_val[slot].astype(jnp.int32).astype(F32) * in_scale[slot]

    r_copies = {}
    n = 0
    for level in range(FAR, 0, -1):
        for d, h in STREAMS:
            if level <= hops(d, h):
                r_copies[(level, d, h)] = (
                    n,
                    remote(out_val.at[n], in_val.at[n], r_send.at[n], r_recv.at[n], at_z(d)),
                    remote(out_scale.at[n], in_scale.at[n], c_send.at[n], c_recv.at[n], at_z(d)),
                )
                n += 1
    x_copies = (
        n,
        remote(out_val.at[n], in_val.at[n], r_send.at[n], r_recv.at[n], x_far),
        remote(out_scale.at[n], in_scale.at[n], c_send.at[n], c_recv.at[n], x_far),
    )

    def post(entry, value):
        slot, data, scale = entry
        encode(value, slot)
        start(data)
        start(scale)

    def fetch(entry):
        slot, data, scale = entry
        data.wait_recv()
        scale.wait_recv()
        return decode(slot)

    def first_send(level, d, h):
        post(r_copies[(level, d, h)], part_of(level * d, h))

    def next_send(level, d, h):
        post(r_copies[(level, d, h)], fetch(r_copies[(level + 1, d, h)]) + part_of(level * d, h))

    def wgrad_tiles(first, last):
        def tile(t, carry):
            at = pl.ds(pl.multiple_of(t * 128, 128), 128)
            wgrad[at, :] = dot_tn(act_all[:, at], aligned[...]).astype(BF16)
            return carry

        lax.fori_loop(first, last, tile, 0)

    sums(0, 2)
    first_send(4, 1, 0)
    first_send(4, -1, 1)
    a_step(3)
    sums(2, 6)
    first_send(3, 1, 1)
    first_send(3, -1, 0)
    next_send(3, 1, 0)
    next_send(3, -1, 1)
    a_step(4)
    own_a.wait()
    sums(6, 10)
    for level in (2, 1):
        next_send(level, 1, 1)
        next_send(level, -1, 0)
        next_send(level, 1, 0)
        next_send(level, -1, 1)
        if level == 2:
            sums(10, 14)
            sums(14, 16)
            wgrad_tiles(0, 2)
        else:
            wgrad_tiles(2, 4)
    away = part_of(0, 1) + fetch(r_copies[(1, 1, 1)])
    away = away + fetch(r_copies[(1, -1, 1)])
    post(x_copies, away)
    home = part_of(0, 0) + fetch(r_copies[(1, -1, 0)])
    home = home + fetch(r_copies[(1, 1, 0)])
    wgrad_tiles(4, 7)
    igrad[...] = (home + fetch(x_copies)).astype(BF16)
    for copy in sent:
        copy.wait_send()


def body(activations, cotangent, down_weight, row_order):
    rows_a, hidden = activations.shape
    rows_g, width = cotangent.shape
    total = row_order.shape[0]
    any_space = pl.BlockSpec(memory_space=pl.ANY)
    vmem = pl.BlockSpec(memory_space=pltpu.VMEM)
    slots = 15
    dma = pltpu.SemaphoreType.DMA
    return pl.pallas_call(
        kernel,
        out_shape=(
            jax.ShapeDtypeStruct((hidden, width), BF16),
            jax.ShapeDtypeStruct((rows_a, hidden), BF16),
        ),
        in_specs=[any_space, any_space, any_space, vmem],
        out_specs=(vmem, vmem),
        scratch_shapes=[
            pltpu.VMEM((total, width), BF16),
            pltpu.VMEM((total, hidden), BF16),
            pltpu.VMEM((hidden, width), BF16),
            pltpu.VMEM((total, 128), F32),
            pltpu.VMEM((total, total), BF16),
            pltpu.VMEM((total, width), BF16),
            pltpu.VMEM((total, hidden), F32),
            pltpu.VMEM((slots, rows_a, hidden), jnp.int16),
            pltpu.VMEM((slots, 1, hidden), F32),
            pltpu.VMEM((slots, rows_a, hidden), jnp.int16),
            pltpu.VMEM((slots, 1, hidden), F32),
            dma((15,)), dma((15,)), dma((16,)), dma((16,)), dma((15,)), dma((15,)),
            dma((15,)), dma((15,)), dma((15,)), dma((15,)), dma((3,)),
        ],
        compiler_params=pltpu.CompilerParams(
            collective_id=0, has_side_effects=True, vmem_limit_bytes=48 * 1024 * 1024
        ),
    )(activations, cotangent, down_weight, row_order.reshape(total // 128, 128))


def solution(mesh):
    in_specs = (P("row", "col"), P("col", "row"), P("col", "row"), P())
    out_specs = (P("col", "row"), P("row", "col"))
    return jax.shard_map(body, mesh=mesh, in_specs=in_specs, out_specs=out_specs, check_vma=False)
```

```python
import jax
import jax.numpy as jnp
from jax import lax
from jax.experimental import pallas as pl
from jax.experimental.pallas import tpu as pltpu
from jax.sharding import PartitionSpec as P

MESH = pl.DeviceIdType.MESH
RING = 8
FAR = RING // 2
GROUPS = [(FAR, 0), (FAR, 1)]
for _d in (3, 2, 1):
    GROUPS += [(_d, 0), (_d, 1), (-_d, 0), (-_d, 1)]
GROUPS += [(0, 0), (0, 1)]
PLACE = {g: i for i, g in enumerate(GROUPS)}
DISTANCES = [4, 3, -3, 2, -2, 1, -1, 0]
SPLIT = 512
F32 = jnp.float32
BF16 = jnp.bfloat16
I16 = jnp.int16


def z_place(distance, half):
    return PLACE[(FAR if abs(distance) == FAR else distance, half)]


def hops(direction, stream):
    return FAR if (direction == 1) == (stream == 0) else FAR - 1


STREAMS = [(d, s) for s in (0, 1) for d in (1, -1)]


def dot_nt(a, b):
    return lax.dot_general(a, b, (((1,), (1,)), ((), ())), preferred_element_type=F32)


def dot_tn(a, b):
    return lax.dot_general(a, b, (((0,), (0,)), ((), ())), preferred_element_type=F32)


def kernel(
    act, cot, weight, order, wgrad, igrad,
    cot_all, act_all, w_vmem, order_vmem, place_col, pick, aligned, partial, wgrad_vmem, igrad_vmem,
    za_out, za_out_s, za_in, za_in_s, xb_out, xb_out_s, xb_in, xb_in_s, zb_out, zb_out_s, zb_in, zb_in_s,
    g_send, g_recv, s_send, s_recv, a_send, a_recv,
    za_sem, xb_sem, zb_sem, local_sem,
):
    row, col = lax.axis_index("row"), lax.axis_index("col")
    xh, z = row // RING, lax.rem(row, RING)
    y, xl, core = col // 4, lax.rem(col, 4) // 2, lax.rem(col, 2)

    def at_z(step):
        return (xh * RING + lax.rem(z + step + RING, RING), col)

    def at_y(step):
        return (row, lax.rem(y + step + RING, RING) * 4 + xl * 2 + core)

    x_far = ((1 - xh) * RING + z, col)
    x_near = (row, y * 4 + (1 - xl) * 2 + core)
    sibling = (row, y * 4 + xl * 2 + 1 - core)

    rows_g = cot.shape[0]
    rows_a, hidden = act.shape
    total = cot_all.shape[0]
    half = total // 2
    rows_h = rows_a // 2

    def g_slot(core_d, y_d, x_d):
        return cot_all.at[pl.ds(core_d * half + ((y_d % RING) * 2 + x_d) * rows_g, rows_g)]

    def g_half(ref, d):
        return ref.at[pl.ds(0 if d == 1 else rows_g // 2, rows_g // 2)]

    def a_rows(distance, h):
        return pl.ds(z_place(distance, h) * rows_a, rows_a)

    def remote(src, dst, send, recv, device):
        return pltpu.make_async_remote_copy(
            src_ref=src, dst_ref=dst, send_sem=send, recv_sem=recv, device_id=device, device_id_type=MESH
        )

    barrier = pltpu.get_barrier_semaphore()
    partners = (at_y(1), at_y(-1), at_y(2), at_y(-2), x_near, sibling, at_z(1), at_z(-1), x_far)
    for device in partners:
        pl.semaphore_signal(barrier, inc=1, device_id=device, device_id_type=MESH)

    own_order = pltpu.make_async_copy(order, order_vmem, local_sem.at[3])
    own_g = pltpu.make_async_copy(cot, g_slot(0, 0, 0), local_sem.at[0])
    own_a = pltpu.make_async_copy(act, act_all.at[a_rows(0, 0)], local_sem.at[1])
    own_w = pltpu.make_async_copy(weight, w_vmem, local_sem.at[2])
    own_order.start()
    own_g.start()
    own_a.start()
    own_w.start()
    pl.semaphore_wait(barrier, len(partners))

    sent = []

    def start(copy):
        copy.start()
        sent.append(copy)
        return copy

    g_count = [0]

    def g_copy(src, dst, device):
        n = g_count[0]
        g_count[0] += 1
        return remote(src, dst, g_send.at[n], g_recv.at[n], device)

    own2 = {d: g_copy(cot, g_slot(0, -2 * d, 0), at_y(2 * d)) for d in (1, -1)}
    own1 = {d: g_copy(cot, g_slot(0, -d, 0), at_y(d)) for d in (1, -1)}
    near0 = g_copy(cot, g_slot(0, 0, 1), x_near)
    near2 = {d: g_copy(g_slot(0, -2 * d, 0), g_slot(0, -2 * d, 1), x_near) for d in (1, -1)}
    far3 = {d: g_copy(g_slot(0, -2 * d, 0), g_slot(0, -3 * d, 0), at_y(d)) for d in (1, -1)}
    far4 = {d: g_copy(g_half(g_slot(0, -2 * d, 0), d), g_half(g_slot(0, FAR, 0), d), at_y(2 * d)) for d in (1, -1)}
    near4 = g_copy(g_slot(0, FAR, 0), g_slot(0, FAR, 1), x_near)
    side1 = {d: g_copy(g_slot(0, 0, 1), g_slot(0, -d, 1), at_y(d)) for d in (1, -1)}
    side3 = {d: g_copy(g_slot(0, -2 * d, 1), g_slot(0, -3 * d, 1), at_y(d)) for d in (1, -1)}
    shared = {}
    for y_d in range(RING):
        for x_d in range(2):
            i = y_d * 2 + x_d
            src = cot if i == 0 else g_slot(0, y_d, x_d)
            shared[(y_d, x_d)] = remote(src, g_slot(1, y_d, x_d), s_send.at[i], s_recv.at[i], sibling)

    def share(y_d, x_d):
        start(shared[(y_d % RING, x_d)])

    a_ring = {}
    n = 0
    for step in range(1, FAR + 1):
        for d, s in STREAMS:
            if step <= hops(d, s):
                src = act if (step == 1 and s == 0) else act_all.at[a_rows(-d * (step - 1), s)]
                a_ring[(step, d, s)] = remote(src, act_all.at[a_rows(-d * step, s)], a_send.at[n], a_recv.at[n], at_z(d))
                n += 1
    a_far = remote(act, act_all.at[a_rows(0, 1)], a_send.at[n], a_recv.at[n], x_far)

    def a_hop(step, s):
        for d in (1, -1):
            if step <= hops(d, s):
                a_ring[(step, d, s)].wait_recv()
                if step < hops(d, s):
                    start(a_ring[(step + 1, d, s)])

    start(own2[1])
    start(own2[-1])
    start(near0)
    start(own1[1])
    start(own1[-1])
    start(a_ring[(1, 1, 0)])
    start(a_ring[(1, -1, 0)])
    start(a_far)
    share(0, 0)

    own_order.wait()
    r = order_vmem[...]
    spot = (
        lax.rem(r // 32 + core, 2) * half
        + lax.rem(r // 128 - y + RING, RING) * (2 * rows_g)
        + lax.rem(r // 64 + xl, 2) * rows_g
        + lax.rem(r, 32)
    ).astype(F32)
    for b in range(total // 128):
        place_col[b * 128:(b + 1) * 128, :] = jnp.transpose(jnp.broadcast_to(spot[b:b + 1, :], (128, 128)))

    lanes = lax.broadcasted_iota(jnp.int32, (rows_a, 128), 1).astype(F32)

    def build_pick(first, last):
        for i in range(first, last):
            distance, h = GROUPS[i]
            shard = lax.rem(xh + h, 2) * RING + lax.rem(z + distance + RING, RING)
            want = place_col[pl.ds(pl.multiple_of(shard * rows_a, rows_a), rows_a), :]
            for j in range(total // 128):
                hit = jnp.where(want == lanes + float(j * 128), 1.0, 0.0).astype(F32)
                pick[i * rows_a:(i + 1) * rows_a, j * 128:(j + 1) * 128] = hit.astype(BF16)

    build_pick(0, 4)
    near0.wait_recv()
    start(side1[1])
    start(side1[-1])
    share(0, 1)
    build_pick(4, 8)
    for d in (1, -1):
        own2[d].wait_recv()
        start(far4[d])
        start(far3[d])
        start(near2[d])
        share(-2 * d, 0)
    a_far.wait_recv()
    start(a_ring[(1, 1, 1)])
    start(a_ring[(1, -1, 1)])
    a_hop(1, 0)
    for d in (1, -1):
        own1[d].wait_recv()
        share(-d, 0)
    build_pick(8, 12)
    for d in (1, -1):
        side1[d].wait_recv()
        share(-d, 1)
    for d in (1, -1):
        near2[d].wait_recv()
        start(side3[d])
        share(-2 * d, 1)
    far4[1].wait_recv()
    far4[-1].wait_recv()
    start(near4)
    share(FAR, 0)
    for d in (1, -1):
        far3[d].wait_recv()
        share(-3 * d, 0)
    build_pick(12, 16)
    a_hop(2, 0)
    a_hop(1, 1)
    for d in (1, -1):
        side3[d].wait_recv()
        share(-3 * d, 1)
    near4.wait_recv()
    share(FAR, 1)
    own_g.wait()
    own_w.wait()
    for key in shared:
        shared[key].wait_recv()

    def sums(first, last):
        rows = slice(first * rows_a, last * rows_a)
        aligned[rows, :] = jnp.dot(pick[rows, :], cot_all[...], preferred_element_type=F32).astype(BF16)
        partial[rows, :] = dot_nt(aligned[rows, :], w_vmem[...])

    def part_a(distance, h):
        i = z_place(distance, h)
        return partial[i * rows_a:(i + 1) * rows_a, :SPLIT]

    def part_b(distance, h):
        i = z_place(distance, h)
        return partial[i * rows_a:(i + 1) * rows_a, SPLIT:]

    def encode(value, out, scale):
        top = jnp.maximum(jnp.max(jnp.abs(value), axis=0, keepdims=True), 1e-34)
        out[...] = jnp.round(value * (32767.0 / top)).astype(jnp.int32).astype(I16)
        scale[...] = top * (1.0 / 32767.0)

    def decode(data, scale):
        return data[...].astype(jnp.int32).astype(F32) * scale[...]

    class Parcel:
        def __init__(self, refs, sems, slot, device, rows=None):
            out, out_s, got, got_s = (ref.at[slot] for ref in refs)
            if rows is not None:
                out, got = out.at[pl.ds(0, rows)], got.at[pl.ds(0, rows)]
            self.out, self.out_s, self.got, self.got_s = out, out_s, got, got_s
            self.data = remote(out, got, sems.at[0, slot], sems.at[1, slot], device)
            self.scale = remote(out_s, got_s, sems.at[2, slot], sems.at[3, slot], device)

        def post(self, value):
            encode(value, self.out, self.out_s)
            start(self.data)
            start(self.scale)

        def fetch(self):
            self.data.wait_recv()
            self.scale.wait_recv()
            return decode(self.got, self.got_s)

    za_refs = (za_out, za_out_s, za_in, za_in_s)
    za = {}
    for level in range(FAR, 0, -1):
        for d, h in STREAMS:
            if level <= hops(d, h):
                za[(level, d, h)] = Parcel(za_refs, za_sem, len(za), at_z(d))
    xa = Parcel(za_refs, za_sem, len(za), x_far)
    xb = {g: Parcel((xb_out, xb_out_s, xb_in, xb_in_s), xb_sem, i, x_far) for i, g in enumerate(DISTANCES)}
    zb = {}
    for level in range(FAR, 0, -1):
        for d in (1, -1):
            rows = rows_h if level == FAR else None
            zb[(level, d)] = Parcel((zb_out, zb_out_s, zb_in, zb_in_s), zb_sem, len(zb), at_z(d), rows)

    def a_first(level, d, h):
        za[(level, d, h)].post(part_a(level * d, h))

    def a_next(level, d, h):
        za[(level, d, h)].post(za[(level + 1, d, h)].fetch() + part_a(level * d, h))

    def b_cross(distance):
        xb[distance].post(part_b(distance, 1))

    def b_first():
        value = part_b(FAR, 0) + xb[FAR].fetch()
        zb[(FAR, 1)].post(value[:rows_h])
        zb[(FAR, -1)].post(value[rows_h:])

    def b_next(level, d):
        value = part_b(level * d, 0) + xb[level * d].fetch()
        got = zb[(level + 1, d)].fetch()
        if level + 1 < FAR:
            value = value + got
        elif d == 1:
            value = jnp.concatenate([value[:rows_h] + got, value[rows_h:]], axis=0)
        else:
            value = jnp.concatenate([value[:rows_h], value[rows_h:] + got], axis=0)
        zb[(level, d)].post(value)

    stored = []

    def wgrad_tiles(first, last):
        def tile(t, carry):
            at = pl.ds(pl.multiple_of(t * 128, 128), 128)
            wgrad_vmem[at, :] = dot_tn(act_all[:, at], aligned[...]).astype(BF16)
            return carry

        lax.fori_loop(first, last, tile, 0)
        rows = pl.ds(first * 128, (last - first) * 128)
        copy = pltpu.make_async_copy(wgrad_vmem.at[rows], wgrad.at[rows], local_sem.at[4 + len(stored)])
        copy.start()
        stored.append(copy)

    sums(0, 2)
    a_first(4, 1, 0)
    a_first(4, -1, 1)
    b_cross(4)
    sums(2, 6)
    a_first(3, 1, 1)
    a_first(3, -1, 0)
    b_cross(3)
    b_cross(-3)
    sums(6, 10)
    b_cross(2)
    b_cross(-2)
    a_next(3, 1, 0)
    a_next(3, -1, 1)
    b_first()
    a_hop(3, 0)
    sums(10, 14)
    b_cross(1)
    b_cross(-1)
    a_next(2, 1, 1)
    a_next(2, -1, 0)
    sums(14, 16)
    b_cross(0)
    b_next(3, 1)
    b_next(3, -1)
    a_next(2, 1, 0)
    a_next(2, -1, 1)
    a_hop(2, 1)
    a_next(1, 1, 1)
    a_next(1, -1, 0)
    a_hop(4, 0)
    b_next(2, 1)
    b_next(2, -1)
    a_next(1, 1, 0)
    a_next(1, -1, 1)
    a_hop(3, 1)
    b_next(1, 1)
    b_next(1, -1)
    a_hop(4, 1)
    own_a.wait()
    wgrad_tiles(0, 2)
    xa.post(part_a(0, 1) + za[(1, 1, 1)].fetch() + za[(1, -1, 1)].fetch())
    home_b = part_b(0, 0) + xb[0].fetch() + zb[(1, 1)].fetch() + zb[(1, -1)].fetch()
    igrad_vmem[:, SPLIT:] = home_b.astype(BF16)
    partial[:rows_a, :SPLIT] = part_a(0, 0) + za[(1, -1, 0)].fetch() + za[(1, 1, 0)].fetch()
    wgrad_tiles(2, 7)
    igrad_vmem[:, :SPLIT] = (partial[:rows_a, :SPLIT] + xa.fetch()).astype(BF16)
    copy = pltpu.make_async_copy(igrad_vmem, igrad, local_sem.at[4 + len(stored)])
    copy.start()
    stored.append(copy)
    for copy in sent:
        copy.wait_send()
    for copy in stored:
        copy.wait()


def body(activations, cotangent, down_weight, row_order):
    rows_a, hidden = activations.shape
    rows_g, width = cotangent.shape
    total = row_order.shape[0]
    hbm = pl.BlockSpec(memory_space=pltpu.HBM)
    dma = pltpu.SemaphoreType.DMA

    def parcels(slots, columns):
        return [
            pltpu.VMEM((slots, rows_a, columns), I16),
            pltpu.VMEM((slots, 1, columns), F32),
            pltpu.VMEM((slots, rows_a, columns), I16),
            pltpu.VMEM((slots, 1, columns), F32),
        ]

    return pl.pallas_call(
        kernel,
        out_shape=(
            jax.ShapeDtypeStruct((hidden, width), BF16),
            jax.ShapeDtypeStruct((rows_a, hidden), BF16),
        ),
        in_specs=[hbm] * 4,
        out_specs=(hbm, hbm),
        scratch_shapes=[
            pltpu.VMEM((total, width), BF16),
            pltpu.VMEM((total, hidden), BF16),
            pltpu.VMEM((hidden, width), BF16),
            pltpu.VMEM((total // 128, 128), jnp.int32),
            pltpu.VMEM((total, 128), F32),
            pltpu.VMEM((total, total), BF16),
            pltpu.VMEM((total, width), BF16),
            pltpu.VMEM((total, hidden), F32),
            pltpu.VMEM((hidden, width), BF16),
            pltpu.VMEM((rows_a, hidden), BF16),
            *parcels(15, SPLIT),
            *parcels(8, hidden - SPLIT),
            *parcels(8, hidden - SPLIT),
            dma((16,)), dma((16,)), dma((16,)), dma((16,)), dma((15,)), dma((15,)),
            dma((4, 15)), dma((4, 8)), dma((4, 8)), dma((8,)),
        ],
        compiler_params=pltpu.CompilerParams(
            collective_id=0, has_side_effects=True, vmem_limit_bytes=62 * 1024 * 1024
        ),
    )(activations, cotangent, down_weight, row_order.reshape(total // 128, 128))


def solution(mesh):
    in_specs = (P("row", "col"), P("col", "row"), P("col", "row"), P())
    out_specs = (P("col", "row"), P("row", "col"))
    return jax.shard_map(body, mesh=mesh, in_specs=in_specs, out_specs=out_specs, check_vma=False)
```

```python
import jax
import jax.numpy as jnp
from jax import lax
from jax.experimental import pallas as pl
from jax.experimental.pallas import tpu as pltpu
from jax.sharding import PartitionSpec as P

MESH = pl.DeviceIdType.MESH
RING = 8
FAR = RING // 2
GROUPS = [(FAR, 0), (FAR, 1)]
for _d in (3, 2, 1):
    GROUPS += [(_d, 0), (_d, 1), (-_d, 0), (-_d, 1)]
GROUPS += [(0, 0), (0, 1)]
PLACE = {g: i for i, g in enumerate(GROUPS)}
DISTANCES = [4, 3, -3, 2, -2, 1, -1, 0]
SPLIT = 512
F32 = jnp.float32
BF16 = jnp.bfloat16
I16 = jnp.int16


def z_place(distance, half):
    return PLACE[(FAR if abs(distance) == FAR else distance, half)]


def hops(direction, stream):
    return FAR if (direction == 1) == (stream == 0) else FAR - 1


STREAMS = [(d, s) for s in (0, 1) for d in (1, -1)]


def dot_nt(a, b):
    return lax.dot_general(a, b, (((1,), (1,)), ((), ())), preferred_element_type=F32)


def dot_tn(a, b):
    return lax.dot_general(a, b, (((0,), (0,)), ((), ())), preferred_element_type=F32)


def kernel(
    act, cot, weight, order, wgrad, igrad,
    cot_all, act_all, w_vmem, order_vmem, place_col, pick, aligned, partial,
    za_out, za_out_s, za_in, za_in_s, xb_out, xb_out_s, xb_in, xb_in_s, zb_out, zb_out_s, zb_in, zb_in_s,
    g_send, g_recv, s_send, s_recv, a_send, a_recv,
    za_sem, xb_sem, zb_sem, local_sem,
):
    row, col = lax.axis_index("row"), lax.axis_index("col")
    xh, z = row // RING, lax.rem(row, RING)
    y, xl, core = col // 4, lax.rem(col, 4) // 2, lax.rem(col, 2)

    def at_z(step):
        return (xh * RING + lax.rem(z + step + RING, RING), col)

    def at_y(step):
        return (row, lax.rem(y + step + RING, RING) * 4 + xl * 2 + core)

    x_far = ((1 - xh) * RING + z, col)
    x_near = (row, y * 4 + (1 - xl) * 2 + core)
    sibling = (row, y * 4 + xl * 2 + 1 - core)

    rows_g = cot.shape[0]
    rows_a, hidden = act.shape
    total = cot_all.shape[0]
    half = total // 2
    rows_h = rows_a // 2

    def g_slot(core_d, y_d, x_d):
        return cot_all.at[pl.ds(core_d * half + ((y_d % RING) * 2 + x_d) * rows_g, rows_g)]

    def g_half(ref, d):
        return ref.at[pl.ds(0 if d == 1 else rows_g // 2, rows_g // 2)]

    def a_rows(distance, h):
        return pl.ds(z_place(distance, h) * rows_a, rows_a)

    def remote(src, dst, send, recv, device):
        return pltpu.make_async_remote_copy(
            src_ref=src, dst_ref=dst, send_sem=send, recv_sem=recv, device_id=device, device_id_type=MESH
        )

    barrier = pltpu.get_barrier_semaphore()
    partners = (at_y(1), at_y(-1), at_y(2), at_y(-2), x_near, sibling, at_z(1), at_z(-1), at_z(2), at_z(-2), x_far)
    for device in partners:
        pl.semaphore_signal(barrier, inc=1, device_id=device, device_id_type=MESH)

    own_order = pltpu.make_async_copy(order, order_vmem, local_sem.at[3])
    own_g = pltpu.make_async_copy(cot, g_slot(0, 0, 0), local_sem.at[0])
    own_a = pltpu.make_async_copy(act, act_all.at[a_rows(0, 0)], local_sem.at[1])
    own_w = pltpu.make_async_copy(weight, w_vmem, local_sem.at[2])
    own_order.start()
    own_g.start()
    own_a.start()
    own_w.start()
    pl.semaphore_wait(barrier, len(partners))

    sent = []

    def start(copy):
        copy.start()
        sent.append(copy)
        return copy

    g_count = [0]

    def g_copy(src, dst, device):
        n = g_count[0]
        g_count[0] += 1
        return remote(src, dst, g_send.at[n], g_recv.at[n], device)

    own2 = {d: g_copy(cot, g_slot(0, -2 * d, 0), at_y(2 * d)) for d in (1, -1)}
    own1 = {d: g_copy(cot, g_slot(0, -d, 0), at_y(d)) for d in (1, -1)}
    near0 = g_copy(cot, g_slot(0, 0, 1), x_near)
    near2 = {d: g_copy(g_slot(0, -2 * d, 0), g_slot(0, -2 * d, 1), x_near) for d in (1, -1)}
    far3 = {d: g_copy(g_slot(0, -2 * d, 0), g_slot(0, -3 * d, 0), at_y(d)) for d in (1, -1)}
    far4 = {d: g_copy(g_half(g_slot(0, -2 * d, 0), d), g_half(g_slot(0, FAR, 0), d), at_y(2 * d)) for d in (1, -1)}
    side1 = {d: g_copy(g_slot(0, 0, 1), g_slot(0, -d, 1), at_y(d)) for d in (1, -1)}
    side3 = {d: g_copy(g_slot(0, -2 * d, 1), g_slot(0, -3 * d, 1), at_y(d)) for d in (1, -1)}
    side4 = {d: g_copy(g_half(g_slot(0, -2 * d, 1), d), g_half(g_slot(0, FAR, 1), d), at_y(2 * d)) for d in (1, -1)}
    shared = {}
    for y_d in range(RING):
        for x_d in range(2):
            i = y_d * 2 + x_d
            src = cot if i == 0 else g_slot(0, y_d, x_d)
            shared[(y_d, x_d)] = remote(src, g_slot(1, y_d, x_d), s_send.at[i], s_recv.at[i], sibling)

    def share(y_d, x_d):
        start(shared[(y_d % RING, x_d)])

    a_ring = {}
    n = 0
    for step in range(1, FAR + 1):
        for d, s in STREAMS:
            if step <= hops(d, s):
                src = act if (step == 1 and s == 0) else act_all.at[a_rows(-d * (step - 1), s)]
                a_ring[(step, d, s)] = remote(src, act_all.at[a_rows(-d * step, s)], a_send.at[n], a_recv.at[n], at_z(d))
                n += 1
    a_far = remote(act, act_all.at[a_rows(0, 1)], a_send.at[n], a_recv.at[n], x_far)

    def a_hop(step, s):
        for d in (1, -1):
            if step <= hops(d, s):
                a_ring[(step, d, s)].wait_recv()
                if step < hops(d, s):
                    start(a_ring[(step + 1, d, s)])

    start(own2[1])
    start(own2[-1])
    start(near0)
    start(own1[1])
    start(own1[-1])
    start(a_ring[(1, 1, 0)])
    start(a_ring[(1, -1, 0)])
    start(a_far)
    share(0, 0)

    own_order.wait()
    r = order_vmem[...]
    spot = (
        lax.rem(r // 32 + core, 2) * half
        + lax.rem(r // 128 - y + RING, RING) * (2 * rows_g)
        + lax.rem(r // 64 + xl, 2) * rows_g
        + lax.rem(r, 32)
    ).astype(F32)
    for b in range(total // 128):
        place_col[b * 128:(b + 1) * 128, :] = jnp.transpose(jnp.broadcast_to(spot[b:b + 1, :], (128, 128)))

    lanes = lax.broadcasted_iota(jnp.int32, (rows_a, 128), 1).astype(F32)

    def build_pick(first, last):
        for i in range(first, last):
            distance, h = GROUPS[i]
            shard = lax.rem(xh + h, 2) * RING + lax.rem(z + distance + RING, RING)
            want = place_col[pl.ds(pl.multiple_of(shard * rows_a, rows_a), rows_a), :]
            for j in range(total // 128):
                hit = jnp.where(want == lanes + float(j * 128), 1.0, 0.0).astype(F32)
                pick[i * rows_a:(i + 1) * rows_a, j * 128:(j + 1) * 128] = hit.astype(BF16)

    build_pick(0, 4)
    near0.wait_recv()
    start(side1[1])
    start(side1[-1])
    share(0, 1)
    build_pick(4, 8)
    for d in (1, -1):
        own2[d].wait_recv()
        start(far4[d])
        start(far3[d])
        start(near2[d])
        share(-2 * d, 0)
    a_hop(1, 0)
    a_far.wait_recv()
    start(a_ring[(1, 1, 1)])
    start(a_ring[(1, -1, 1)])
    for d in (1, -1):
        own1[d].wait_recv()
        share(-d, 0)
    build_pick(8, 12)
    for d in (1, -1):
        side1[d].wait_recv()
        share(-d, 1)
    for d in (1, -1):
        near2[d].wait_recv()
        start(side4[d])
        start(side3[d])
        share(-2 * d, 1)
    a_hop(2, 0)
    far4[1].wait_recv()
    far4[-1].wait_recv()
    share(FAR, 0)
    for d in (1, -1):
        far3[d].wait_recv()
        share(-3 * d, 0)
    build_pick(12, 16)
    a_hop(1, 1)
    for d in (1, -1):
        side3[d].wait_recv()
        share(-3 * d, 1)
    side4[1].wait_recv()
    side4[-1].wait_recv()
    share(FAR, 1)
    a_hop(3, 0)
    own_g.wait()
    own_w.wait()
    for key in shared:
        shared[key].wait_recv()

    def sums(first, last):
        rows = slice(first * rows_a, last * rows_a)
        aligned[rows, :] = jnp.dot(pick[rows, :], cot_all[...], preferred_element_type=F32).astype(BF16)
        partial[rows, :] = dot_nt(aligned[rows, :], w_vmem[...])

    def part_a(distance, h):
        i = z_place(distance, h)
        return partial[i * rows_a:(i + 1) * rows_a, :SPLIT]

    def part_b(distance, h):
        i = z_place(distance, h)
        return partial[i * rows_a:(i + 1) * rows_a, SPLIT:]

    def encode(value, out, scale):
        top = jnp.maximum(jnp.max(jnp.abs(value), axis=0, keepdims=True), 1e-34)
        out[...] = jnp.round(value * (32767.0 / top)).astype(jnp.int32).astype(I16)
        scale[...] = top * (1.0 / 32767.0)

    def decode(data, scale):
        return data[...].astype(jnp.int32).astype(F32) * scale[...]

    class Parcel:
        def __init__(self, refs, sems, slot, device, rows=None):
            out, out_s, got, got_s = (ref.at[slot] for ref in refs)
            if rows is not None:
                out, got = out.at[pl.ds(0, rows)], got.at[pl.ds(0, rows)]
            self.out, self.out_s, self.got, self.got_s = out, out_s, got, got_s
            self.data = remote(out, got, sems.at[0, slot], sems.at[1, slot], device)
            self.scale = remote(out_s, got_s, sems.at[2, slot], sems.at[3, slot], device)

        def post(self, value):
            encode(value, self.out, self.out_s)
            start(self.data)
            start(self.scale)

        def fetch(self):
            self.data.wait_recv()
            self.scale.wait_recv()
            return decode(self.got, self.got_s)

    za_refs = (za_out, za_out_s, za_in, za_in_s)
    za = {}
    for level in range(FAR, 0, -1):
        for d, h in STREAMS:
            if level <= hops(d, h):
                za[(level, d, h)] = Parcel(za_refs, za_sem, len(za), at_z(d))
    xa = Parcel(za_refs, za_sem, len(za), x_far)
    xb = {g: Parcel((xb_out, xb_out_s, xb_in, xb_in_s), xb_sem, i, x_far) for i, g in enumerate(DISTANCES)}
    zb = {}
    for level in range(FAR, 0, -1):
        for d in (1, -1):
            rows = rows_h if level == FAR else None
            zb[(level, d)] = Parcel((zb_out, zb_out_s, zb_in, zb_in_s), zb_sem, len(zb), at_z(d), rows)

    def a_first(level, d, h):
        za[(level, d, h)].post(part_a(level * d, h))

    def a_next(level, d, h):
        za[(level, d, h)].post(za[(level + 1, d, h)].fetch() + part_a(level * d, h))

    def b_cross(distance):
        xb[distance].post(part_b(distance, 1))

    def b_first():
        value = part_b(FAR, 0) + xb[FAR].fetch()
        zb[(FAR, 1)].post(value[:rows_h])
        zb[(FAR, -1)].post(value[rows_h:])

    def b_next(level, d):
        value = part_b(level * d, 0) + xb[level * d].fetch()
        got = zb[(level + 1, d)].fetch()
        if level + 1 < FAR:
            value = value + got
        elif d == 1:
            value = jnp.concatenate([value[:rows_h] + got, value[rows_h:]], axis=0)
        else:
            value = jnp.concatenate([value[:rows_h], value[rows_h:] + got], axis=0)
        zb[(level, d)].post(value)

    def wgrad_tiles(first, last):
        def tile(t, carry):
            at = pl.ds(pl.multiple_of(t * 128, 128), 128)
            wgrad[at, :] = dot_tn(act_all[:, at], aligned[...]).astype(BF16)
            return carry

        lax.fori_loop(first, last, tile, 0)

    sums(0, 2)
    a_first(4, -1, 1)
    a_first(4, 1, 0)
    b_cross(4)
    sums(2, 6)
    a_first(3, 1, 1)
    a_first(3, -1, 0)
    b_cross(3)
    b_cross(-3)
    a_hop(2, 1)
    a_next(3, -1, 1)
    a_next(3, 1, 0)
    sums(6, 10)
    b_first()
    b_cross(2)
    b_cross(-2)
    a_next(2, 1, 1)
    a_next(2, -1, 0)
    sums(10, 16)
    b_next(3, 1)
    b_next(3, -1)
    b_cross(1)
    b_cross(-1)
    a_next(2, -1, 1)
    a_next(2, 1, 0)
    a_hop(3, 1)
    a_next(1, 1, 1)
    a_next(1, -1, 0)
    b_next(2, 1)
    b_next(2, -1)
    b_cross(0)
    a_next(1, -1, 1)
    a_next(1, 1, 0)
    a_hop(4, 0)
    a_hop(4, 1)
    own_a.wait()
    b_next(1, 1)
    b_next(1, -1)
    wgrad_tiles(0, 2)
    xa.post(part_a(0, 1) + za[(1, 1, 1)].fetch() + za[(1, -1, 1)].fetch())
    wgrad_tiles(2, 5)
    partial[:rows_a, :SPLIT] = part_a(0, 0) + za[(1, -1, 0)].fetch() + za[(1, 1, 0)].fetch()
    home_b = part_b(0, 0) + xb[0].fetch() + zb[(1, 1)].fetch() + zb[(1, -1)].fetch()
    igrad[:, SPLIT:] = home_b.astype(BF16)
    wgrad_tiles(5, 7)
    igrad[:, :SPLIT] = (partial[:rows_a, :SPLIT] + xa.fetch()).astype(BF16)
    for copy in sent:
        copy.wait_send()


def body(activations, cotangent, down_weight, row_order):
    rows_a, hidden = activations.shape
    rows_g, width = cotangent.shape
    total = row_order.shape[0]
    hbm = pl.BlockSpec(memory_space=pltpu.HBM)
    dma = pltpu.SemaphoreType.DMA

    def parcels(slots, columns):
        return [
            pltpu.VMEM((slots, rows_a, columns), I16),
            pltpu.VMEM((slots, 1, columns), F32),
            pltpu.VMEM((slots, rows_a, columns), I16),
            pltpu.VMEM((slots, 1, columns), F32),
        ]

    operands = (activations, cotangent, down_weight, row_order.reshape(total // 128, 128))
    return pl.pallas_call(
        kernel,
        out_shape=(
            jax.ShapeDtypeStruct((hidden, width), BF16),
            jax.ShapeDtypeStruct((rows_a, hidden), BF16),
        ),
        in_specs=[hbm] * 4,
        out_specs=(pl.BlockSpec(memory_space=pltpu.VMEM),) * 2,
        scratch_shapes=[
            pltpu.VMEM((total, width), BF16),
            pltpu.VMEM((total, hidden), BF16),
            pltpu.VMEM((hidden, width), BF16),
            pltpu.VMEM((total // 128, 128), jnp.int32),
            pltpu.VMEM((total, 128), F32),
            pltpu.VMEM((total, total), BF16),
            pltpu.VMEM((total, width), BF16),
            pltpu.VMEM((total, hidden), F32),
            *parcels(15, SPLIT),
            *parcels(8, hidden - SPLIT),
            *parcels(8, hidden - SPLIT),
            dma((17,)), dma((17,)), dma((16,)), dma((16,)), dma((15,)), dma((15,)),
            dma((4, 15)), dma((4, 8)), dma((4, 8)), dma((4,)),
        ],
        compiler_params=pltpu.CompilerParams(
            collective_id=0, has_side_effects=True, vmem_limit_bytes=40 * 1024 * 1024
        ),
    )(*(pltpu.with_memory_space_constraint(x, pltpu.HBM) for x in operands))


def solution(mesh):
    in_specs = (P("row", "col"), P("col", "row"), P("col", "row"), P())
    out_specs = (P("col", "row"), P("row", "col"))
    return jax.shard_map(body, mesh=mesh, in_specs=in_specs, out_specs=out_specs, check_vma=False)
```

```python
import jax
import jax.numpy as jnp
from jax import lax
from jax.experimental import pallas as pl
from jax.experimental.pallas import tpu as pltpu
from jax.sharding import PartitionSpec as P

MESH = pl.DeviceIdType.MESH
RING = 8
FAR = RING // 2
GROUPS = [(FAR, 0), (FAR, 1)]
for _d in (3, 2, 1):
    GROUPS += [(_d, 0), (_d, 1), (-_d, 0), (-_d, 1)]
GROUPS += [(0, 0), (0, 1)]
PLACE = {g: i for i, g in enumerate(GROUPS)}
DISTANCES = [4, 3, -3, 2, -2, 1, -1, 0]
SPLIT = 256
F32 = jnp.float32
BF16 = jnp.bfloat16
I16 = jnp.int16


def z_place(distance, half):
    return PLACE[(FAR if abs(distance) == FAR else distance, half)]


def hops(direction, stream):
    return FAR if (direction == 1) == (stream == 0) else FAR - 1


STREAMS = [(d, s) for s in (0, 1) for d in (1, -1)]


def dot_nt(a, b):
    return lax.dot_general(a, b, (((1,), (1,)), ((), ())), preferred_element_type=F32)


def dot_tn(a, b):
    return lax.dot_general(a, b, (((0,), (0,)), ((), ())), preferred_element_type=F32)


def kernel(
    act, cot, weight, order, wgrad, igrad,
    cot_all, act_all, w_vmem, order_vmem, place_col, pick, aligned, partial,
    za_out, za_out_s, za_in, za_in_s, xb_out, xb_out_s, xb_in, xb_in_s, zb_out, zb_out_s, zb_in, zb_in_s,
    g_send, g_recv, s_send, s_recv, a_send, a_recv,
    za_sem, xb_sem, zb_sem, local_sem,
):
    row, col = lax.axis_index("row"), lax.axis_index("col")
    xh, z = row // RING, lax.rem(row, RING)
    y, xl, core = col // 4, lax.rem(col, 4) // 2, lax.rem(col, 2)

    def at_z(step):
        return (xh * RING + lax.rem(z + step + RING, RING), col)

    def at_y(step):
        return (row, lax.rem(y + step + RING, RING) * 4 + xl * 2 + core)

    x_far = ((1 - xh) * RING + z, col)
    x_near = (row, y * 4 + (1 - xl) * 2 + core)
    sibling = (row, y * 4 + xl * 2 + 1 - core)

    rows_g = cot.shape[0]
    rows_a, hidden = act.shape
    total = cot_all.shape[0]
    half = total // 2
    rows_h = rows_a // 2

    def g_slot(core_d, y_d, x_d):
        return cot_all.at[pl.ds(core_d * half + ((y_d % RING) * 2 + x_d) * rows_g, rows_g)]

    def g_half(ref, d):
        return ref.at[pl.ds(0 if d == 1 else rows_g // 2, rows_g // 2)]

    def a_rows(distance, h):
        return pl.ds(z_place(distance, h) * rows_a, rows_a)

    def remote(src, dst, send, recv, device):
        return pltpu.make_async_remote_copy(
            src_ref=src, dst_ref=dst, send_sem=send, recv_sem=recv, device_id=device, device_id_type=MESH
        )

    barrier = pltpu.get_barrier_semaphore()
    partners = (at_y(1), at_y(-1), at_y(2), at_y(-2), x_near, sibling, at_z(1), at_z(-1), at_z(2), at_z(-2), x_far)
    for device in partners:
        pl.semaphore_signal(barrier, inc=1, device_id=device, device_id_type=MESH)

    own_order = pltpu.make_async_copy(order, order_vmem, local_sem.at[3])
    own_g = pltpu.make_async_copy(cot, g_slot(0, 0, 0), local_sem.at[0])
    own_a = pltpu.make_async_copy(act, act_all.at[a_rows(0, 0)], local_sem.at[1])
    own_w = pltpu.make_async_copy(weight, w_vmem, local_sem.at[2])
    own_order.start()
    own_g.start()
    own_a.start()
    own_w.start()
    pl.semaphore_wait(barrier, len(partners))

    sent = []

    def start(copy):
        copy.start()
        sent.append(copy)
        return copy

    g_count = [0]

    def g_copy(src, dst, device):
        n = g_count[0]
        g_count[0] += 1
        return remote(src, dst, g_send.at[n], g_recv.at[n], device)

    own2 = {d: g_copy(cot, g_slot(0, -2 * d, 0), at_y(2 * d)) for d in (1, -1)}
    own1 = {d: g_copy(cot, g_slot(0, -d, 0), at_y(d)) for d in (1, -1)}
    near0 = g_copy(cot, g_slot(0, 0, 1), x_near)
    near2 = {d: g_copy(g_slot(0, -2 * d, 0), g_slot(0, -2 * d, 1), x_near) for d in (1, -1)}
    far3 = {d: g_copy(g_slot(0, -2 * d, 0), g_slot(0, -3 * d, 0), at_y(d)) for d in (1, -1)}
    far4 = {d: g_copy(g_half(g_slot(0, -2 * d, 0), d), g_half(g_slot(0, FAR, 0), d), at_y(2 * d)) for d in (1, -1)}
    side1 = {d: g_copy(g_slot(0, 0, 1), g_slot(0, -d, 1), at_y(d)) for d in (1, -1)}
    side3 = {d: g_copy(g_slot(0, -2 * d, 1), g_slot(0, -3 * d, 1), at_y(d)) for d in (1, -1)}
    side4 = {d: g_copy(g_half(g_slot(0, -2 * d, 1), d), g_half(g_slot(0, FAR, 1), d), at_y(2 * d)) for d in (1, -1)}
    shared = {}
    for y_d in range(RING):
        for x_d in range(2):
            i = y_d * 2 + x_d
            src = cot if i == 0 else g_slot(0, y_d, x_d)
            shared[(y_d, x_d)] = remote(src, g_slot(1, y_d, x_d), s_send.at[i], s_recv.at[i], sibling)

    def share(y_d, x_d):
        start(shared[(y_d % RING, x_d)])

    a_ring = {}
    n = 0
    for step in range(1, FAR + 1):
        for d, s in STREAMS:
            if step <= hops(d, s):
                src = act if (step == 1 and s == 0) else act_all.at[a_rows(-d * (step - 1), s)]
                a_ring[(step, d, s)] = remote(src, act_all.at[a_rows(-d * step, s)], a_send.at[n], a_recv.at[n], at_z(d))
                n += 1
    a_far = remote(act, act_all.at[a_rows(0, 1)], a_send.at[n], a_recv.at[n], x_far)

    def a_hop(step, s):
        for d in (1, -1):
            if step <= hops(d, s):
                a_ring[(step, d, s)].wait_recv()
                if step < hops(d, s):
                    start(a_ring[(step + 1, d, s)])

    start(own2[1])
    start(own2[-1])
    start(near0)
    start(own1[1])
    start(own1[-1])
    start(a_ring[(1, 1, 0)])
    start(a_ring[(1, -1, 0)])
    start(a_far)
    share(0, 0)

    own_order.wait()
    r = order_vmem[...]
    spot = (
        lax.rem(r // 32 + core, 2) * half
        + lax.rem(r // 128 - y + RING, RING) * (2 * rows_g)
        + lax.rem(r // 64 + xl, 2) * rows_g
        + lax.rem(r, 32)
    ).astype(F32)
    for b in range(total // 128):
        place_col[b * 128:(b + 1) * 128, :] = jnp.transpose(jnp.broadcast_to(spot[b:b + 1, :], (128, 128)))

    lanes = lax.broadcasted_iota(jnp.int32, (rows_a, 128), 1).astype(F32)

    def build_pick(first, last):
        for i in range(first, last):
            distance, h = GROUPS[i]
            shard = lax.rem(xh + h, 2) * RING + lax.rem(z + distance + RING, RING)
            want = place_col[pl.ds(pl.multiple_of(shard * rows_a, rows_a), rows_a), :]
            for j in range(total // 128):
                hit = jnp.where(want == lanes + float(j * 128), 1.0, 0.0).astype(F32)
                pick[i * rows_a:(i + 1) * rows_a, j * 128:(j + 1) * 128] = hit.astype(BF16)

    build_pick(0, 4)
    near0.wait_recv()
    start(side1[1])
    start(side1[-1])
    share(0, 1)
    build_pick(4, 8)
    for d in (1, -1):
        own2[d].wait_recv()
        start(far4[d])
        start(far3[d])
        start(near2[d])
        share(-2 * d, 0)
    a_hop(1, 0)
    a_far.wait_recv()
    start(a_ring[(1, 1, 1)])
    start(a_ring[(1, -1, 1)])
    for d in (1, -1):
        own1[d].wait_recv()
        share(-d, 0)
    build_pick(8, 12)
    for d in (1, -1):
        side1[d].wait_recv()
        share(-d, 1)
    for d in (1, -1):
        near2[d].wait_recv()
        start(side4[d])
        start(side3[d])
        share(-2 * d, 1)
    a_hop(2, 0)
    far4[1].wait_recv()
    far4[-1].wait_recv()
    share(FAR, 0)
    for d in (1, -1):
        far3[d].wait_recv()
        share(-3 * d, 0)
    build_pick(12, 16)
    a_hop(1, 1)
    for d in (1, -1):
        side3[d].wait_recv()
        share(-3 * d, 1)
    side4[1].wait_recv()
    side4[-1].wait_recv()
    share(FAR, 1)
    a_hop(3, 0)
    own_g.wait()
    own_w.wait()
    for key in shared:
        shared[key].wait_recv()

    def sums(first, last):
        rows = slice(first * rows_a, last * rows_a)
        aligned[rows, :] = jnp.dot(pick[rows, :], cot_all[...], preferred_element_type=F32).astype(BF16)
        partial[rows, :] = dot_nt(aligned[rows, :], w_vmem[...])

    def part_a(distance, h):
        i = z_place(distance, h)
        return partial[i * rows_a:(i + 1) * rows_a, :SPLIT]

    def part_b(distance, h):
        i = z_place(distance, h)
        return partial[i * rows_a:(i + 1) * rows_a, SPLIT:]

    def encode(value, out, scale):
        top = jnp.maximum(jnp.max(jnp.abs(value), axis=0, keepdims=True), 1e-34)
        out[...] = jnp.round(value * (32767.0 / top)).astype(jnp.int32).astype(I16)
        scale[...] = top * (1.0 / 32767.0)

    def decode(data, scale):
        return data[...].astype(jnp.int32).astype(F32) * scale[...]

    class Parcel:
        def __init__(self, refs, sems, slot, device, rows=None):
            out, out_s, got, got_s = (ref.at[slot] for ref in refs)
            if rows is not None:
                out, got = out.at[pl.ds(0, rows)], got.at[pl.ds(0, rows)]
            self.out, self.out_s, self.got, self.got_s = out, out_s, got, got_s
            self.data = remote(out, got, sems.at[0, slot], sems.at[1, slot], device)
            self.scale = remote(out_s, got_s, sems.at[2, slot], sems.at[3, slot], device)

        def post(self, value):
            encode(value, self.out, self.out_s)
            start(self.data)
            start(self.scale)

        def fetch(self):
            self.data.wait_recv()
            self.scale.wait_recv()
            return decode(self.got, self.got_s)

    za_refs = (za_out, za_out_s, za_in, za_in_s)
    za = {}
    for level in range(FAR, 0, -1):
        for d, h in STREAMS:
            if level <= hops(d, h):
                za[(level, d, h)] = Parcel(za_refs, za_sem, len(za), at_z(d))
    xa = Parcel(za_refs, za_sem, len(za), x_far)
    xb = {g: Parcel((xb_out, xb_out_s, xb_in, xb_in_s), xb_sem, i, x_far) for i, g in enumerate(DISTANCES)}
    zb = {}
    for level in range(FAR, 0, -1):
        for d in (1, -1):
            rows = rows_h if level == FAR else None
            zb[(level, d)] = Parcel((zb_out, zb_out_s, zb_in, zb_in_s), zb_sem, len(zb), at_z(2 * d if level == FAR else d), rows)

    def a_first(level, d, h):
        za[(level, d, h)].post(part_a(level * d, h))

    def a_next(level, d, h):
        za[(level, d, h)].post(za[(level + 1, d, h)].fetch() + part_a(level * d, h))

    def b_cross(distance):
        xb[distance].post(part_b(distance, 1))

    def b_first():
        value = part_b(FAR, 0) + xb[FAR].fetch()
        zb[(FAR, 1)].post(value[:rows_h])
        zb[(FAR, -1)].post(value[rows_h:])

    def b_next(level, d):
        value = part_b(level * d, 0) + xb[level * d].fetch()
        if level < 3:
            value = value + zb[(level + 1, d)].fetch()
        if level == 2:
            got = zb[(FAR, d)].fetch()
            if d == 1:
                value = jnp.concatenate([value[:rows_h] + got, value[rows_h:]], axis=0)
            else:
                value = jnp.concatenate([value[:rows_h], value[rows_h:] + got], axis=0)
        zb[(level, d)].post(value)

    def wgrad_tiles(first, last):
        def tile(t, carry):
            at = pl.ds(pl.multiple_of(t * 128, 128), 128)
            wgrad[at, :] = dot_tn(act_all[:, at], aligned[...]).astype(BF16)
            return carry

        lax.fori_loop(first, last, tile, 0)

    sums(0, 2)
    b_cross(4)
    a_first(4, -1, 1)
    a_first(4, 1, 0)
    sums(2, 6)
    b_cross(3)
    b_cross(-3)
    a_first(3, 1, 1)
    a_first(3, -1, 0)
    a_hop(2, 1)
    sums(6, 10)
    b_cross(2)
    b_cross(-2)
    b_first()
    a_next(3, -1, 1)
    a_next(3, 1, 0)
    sums(10, 16)
    b_next(3, 1)
    b_next(3, -1)
    b_cross(1)
    b_cross(-1)
    a_next(2, 1, 1)
    a_next(2, -1, 0)
    a_next(2, -1, 1)
    a_next(2, 1, 0)
    a_hop(3, 1)
    b_next(2, 1)
    b_next(2, -1)
    b_cross(0)
    a_next(1, 1, 1)
    a_next(1, -1, 0)
    a_next(1, -1, 1)
    a_next(1, 1, 0)
    b_next(1, 1)
    b_next(1, -1)
    a_hop(4, 0)
    a_hop(4, 1)
    own_a.wait()
    xa.post(part_a(0, 1) + za[(1, 1, 1)].fetch() + za[(1, -1, 1)].fetch())
    wgrad_tiles(0, 7)
    home_a = part_a(0, 0) + za[(1, -1, 0)].fetch() + za[(1, 1, 0)].fetch() + xa.fetch()
    igrad[:, :SPLIT] = home_a.astype(BF16)
    home_b = part_b(0, 0) + xb[0].fetch() + zb[(1, 1)].fetch() + zb[(1, -1)].fetch()
    igrad[:, SPLIT:] = home_b.astype(BF16)
    for copy in sent:
        copy.wait_send()


def body(activations, cotangent, down_weight, row_order):
    rows_a, hidden = activations.shape
    rows_g, width = cotangent.shape
    total = row_order.shape[0]
    hbm = pl.BlockSpec(memory_space=pltpu.HBM)
    dma = pltpu.SemaphoreType.DMA

    def parcels(slots, columns):
        return [
            pltpu.VMEM((slots, rows_a, columns), I16),
            pltpu.VMEM((slots, 1, columns), F32),
            pltpu.VMEM((slots, rows_a, columns), I16),
            pltpu.VMEM((slots, 1, columns), F32),
        ]

    operands = (activations, cotangent, down_weight, row_order.reshape(total // 128, 128))
    return pl.pallas_call(
        kernel,
        out_shape=(
            jax.ShapeDtypeStruct((hidden, width), BF16),
            jax.ShapeDtypeStruct((rows_a, hidden), BF16),
        ),
        in_specs=[hbm] * 4,
        out_specs=(pl.BlockSpec(memory_space=pltpu.VMEM),) * 2,
        scratch_shapes=[
            pltpu.VMEM((total, width), BF16),
            pltpu.VMEM((total, hidden), BF16),
            pltpu.VMEM((hidden, width), BF16),
            pltpu.VMEM((total // 128, 128), jnp.int32),
            pltpu.VMEM((total, 128), F32),
            pltpu.VMEM((total, total), BF16),
            pltpu.VMEM((total, width), BF16),
            pltpu.VMEM((total, hidden), F32),
            *parcels(15, SPLIT),
            *parcels(8, hidden - SPLIT),
            *parcels(8, hidden - SPLIT),
            dma((17,)), dma((17,)), dma((16,)), dma((16,)), dma((15,)), dma((15,)),
            dma((4, 15)), dma((4, 8)), dma((4, 8)), dma((4,)),
        ],
        compiler_params=pltpu.CompilerParams(
            collective_id=0, has_side_effects=True, vmem_limit_bytes=40 * 1024 * 1024
        ),
    )(*(pltpu.with_memory_space_constraint(x, pltpu.HBM) for x in operands))


def solution(mesh):
    in_specs = (P("row", "col"), P("col", "row"), P("col", "row"), P())
    out_specs = (P("col", "row"), P("row", "col"))
    return jax.shard_map(body, mesh=mesh, in_specs=in_specs, out_specs=out_specs, check_vma=False)
```

```python
import jax
import jax.numpy as jnp
from jax import lax
from jax.experimental import pallas as pl
from jax.experimental.pallas import tpu as pltpu
from jax.sharding import PartitionSpec as P

MESH = pl.DeviceIdType.MESH
RING = 8
FAR = RING // 2
GROUPS = [(FAR, 0), (FAR, 1)]
for _d in (3, 2, 1):
    GROUPS += [(_d, 0), (_d, 1), (-_d, 0), (-_d, 1)]
GROUPS += [(0, 0), (0, 1)]
PLACE = {g: i for i, g in enumerate(GROUPS)}
DISTANCES = [4, 3, -3, 2, -2, 1, -1, 0]
SPLIT = 256
F32 = jnp.float32
BF16 = jnp.bfloat16
I16 = jnp.int16


def z_place(distance, half):
    return PLACE[(FAR if abs(distance) == FAR else distance, half)]


def hops(direction, stream):
    return FAR if (direction == 1) == (stream == 0) else FAR - 1


STREAMS = [(d, s) for s in (0, 1) for d in (1, -1)]


def dot_nt(a, b):
    return lax.dot_general(a, b, (((1,), (1,)), ((), ())), preferred_element_type=F32)


def dot_tn(a, b):
    return lax.dot_general(a, b, (((0,), (0,)), ((), ())), preferred_element_type=F32)


def kernel(
    act, cot, weight, order, wgrad, igrad,
    cot_all, act_all, w_vmem, order_vmem, place_col, pick, aligned, partial,
    za_out, za_out_s, za_in, za_in_s, xb_out, xb_out_s, xb_in, xb_in_s, zb_out, zb_out_s, zb_in, zb_in_s,
    g_send, g_recv, s_send, s_recv, a_send, a_recv,
    za_sem, xb_sem, zb_sem, local_sem,
):
    row, col = lax.axis_index("row"), lax.axis_index("col")
    xh, z = row // RING, lax.rem(row, RING)
    y, xl, core = col // 4, lax.rem(col, 4) // 2, lax.rem(col, 2)

    def at_z(step):
        return (xh * RING + lax.rem(z + step + RING, RING), col)

    def at_y(step):
        return (row, lax.rem(y + step + RING, RING) * 4 + xl * 2 + core)

    x_far = ((1 - xh) * RING + z, col)
    x_near = (row, y * 4 + (1 - xl) * 2 + core)
    sibling = (row, y * 4 + xl * 2 + 1 - core)

    rows_g = cot.shape[0]
    rows_a, hidden = act.shape
    total = cot_all.shape[0]
    half = total // 2
    rows_h = rows_a // 2

    def g_slot(core_d, y_d, x_d):
        return cot_all.at[pl.ds(core_d * half + ((y_d % RING) * 2 + x_d) * rows_g, rows_g)]

    def g_half(ref, d):
        return ref.at[pl.ds(0 if d == 1 else rows_g // 2, rows_g // 2)]

    def a_rows(distance, h):
        return pl.ds(z_place(distance, h) * rows_a, rows_a)

    def remote(src, dst, send, recv, device):
        return pltpu.make_async_remote_copy(
            src_ref=src, dst_ref=dst, send_sem=send, recv_sem=recv, device_id=device, device_id_type=MESH
        )

    barrier = pltpu.get_barrier_semaphore()
    partners = (at_y(1), at_y(-1), at_y(2), at_y(-2), x_near, sibling, at_z(1), at_z(-1), at_z(2), at_z(-2), x_far)
    for device in partners:
        pl.semaphore_signal(barrier, inc=1, device_id=device, device_id_type=MESH)

    own_order = pltpu.make_async_copy(order, order_vmem, local_sem.at[3])
    own_g = pltpu.make_async_copy(cot, g_slot(0, 0, 0), local_sem.at[0])
    own_a = pltpu.make_async_copy(act, act_all.at[a_rows(0, 0)], local_sem.at[1])
    own_w = pltpu.make_async_copy(weight, w_vmem, local_sem.at[2])
    own_order.start()
    own_g.start()
    own_a.start()
    own_w.start()
    pl.semaphore_wait(barrier, len(partners))

    sent = []

    def start(copy):
        copy.start()
        sent.append(copy)
        return copy

    g_count = [0]

    def g_copy(src, dst, device):
        n = g_count[0]
        g_count[0] += 1
        return remote(src, dst, g_send.at[n], g_recv.at[n], device)

    own2 = {d: g_copy(cot, g_slot(0, -2 * d, 0), at_y(2 * d)) for d in (1, -1)}
    own1 = {d: g_copy(cot, g_slot(0, -d, 0), at_y(d)) for d in (1, -1)}
    near0 = g_copy(cot, g_slot(0, 0, 1), x_near)
    near2 = {d: g_copy(g_slot(0, -2 * d, 0), g_slot(0, -2 * d, 1), x_near) for d in (1, -1)}
    far3 = {d: g_copy(g_slot(0, -2 * d, 0), g_slot(0, -3 * d, 0), at_y(d)) for d in (1, -1)}
    far4 = {d: g_copy(g_half(g_slot(0, -2 * d, 0), d), g_half(g_slot(0, FAR, 0), d), at_y(2 * d)) for d in (1, -1)}
    side1 = {d: g_copy(g_slot(0, 0, 1), g_slot(0, -d, 1), at_y(d)) for d in (1, -1)}
    side3 = {d: g_copy(g_slot(0, -2 * d, 1), g_slot(0, -3 * d, 1), at_y(d)) for d in (1, -1)}
    side4 = {d: g_copy(g_half(g_slot(0, -2 * d, 1), d), g_half(g_slot(0, FAR, 1), d), at_y(2 * d)) for d in (1, -1)}
    shared = {}
    for y_d in range(RING):
        for x_d in range(2):
            i = y_d * 2 + x_d
            src = cot if i == 0 else g_slot(0, y_d, x_d)
            shared[(y_d, x_d)] = remote(src, g_slot(1, y_d, x_d), s_send.at[i], s_recv.at[i], sibling)

    def share(y_d, x_d):
        start(shared[(y_d % RING, x_d)])

    a_ring = {}
    n = 0
    for step in range(1, FAR + 1):
        for d, s in STREAMS:
            if step <= hops(d, s):
                src = act if (step == 1 and s == 0) else act_all.at[a_rows(-d * (step - 1), s)]
                a_ring[(step, d, s)] = remote(src, act_all.at[a_rows(-d * step, s)], a_send.at[n], a_recv.at[n], at_z(d))
                n += 1
    a_far = remote(act, act_all.at[a_rows(0, 1)], a_send.at[n], a_recv.at[n], x_far)

    def a_hop(step, s):
        for d in (1, -1):
            if step <= hops(d, s):
                a_ring[(step, d, s)].wait_recv()
                if step < hops(d, s):
                    start(a_ring[(step + 1, d, s)])

    start(own2[1])
    start(own2[-1])
    start(near0)
    start(own1[1])
    start(own1[-1])
    start(a_ring[(1, 1, 0)])
    start(a_ring[(1, -1, 0)])
    start(a_far)
    share(0, 0)

    own_order.wait()
    r = order_vmem[...]
    spot = (
        lax.rem(r // 32 + core, 2) * half
        + lax.rem(r // 128 - y + RING, RING) * (2 * rows_g)
        + lax.rem(r // 64 + xl, 2) * rows_g
        + lax.rem(r, 32)
    ).astype(F32)
    for b in range(total // 128):
        place_col[b * 128:(b + 1) * 128, :] = jnp.transpose(jnp.broadcast_to(spot[b:b + 1, :], (128, 128)))

    lanes = lax.broadcasted_iota(jnp.int32, (rows_a, 128), 1).astype(F32)

    def build_pick(first, last):
        for i in range(first, last):
            distance, h = GROUPS[i]
            shard = lax.rem(xh + h, 2) * RING + lax.rem(z + distance + RING, RING)
            want = place_col[pl.ds(pl.multiple_of(shard * rows_a, rows_a), rows_a), :]
            for j in range(total // 128):
                hit = jnp.where(want == lanes + float(j * 128), 1.0, 0.0).astype(F32)
                pick[i * rows_a:(i + 1) * rows_a, j * 128:(j + 1) * 128] = hit.astype(BF16)

    build_pick(0, 4)
    near0.wait_recv()
    start(side1[1])
    start(side1[-1])
    share(0, 1)
    build_pick(4, 8)
    for d in (1, -1):
        own2[d].wait_recv()
        start(near2[d])
        start(far4[d])
        start(far3[d])
        share(-2 * d, 0)
    a_hop(1, 0)
    a_far.wait_recv()
    start(a_ring[(1, 1, 1)])
    start(a_ring[(1, -1, 1)])
    for d in (1, -1):
        own1[d].wait_recv()
        share(-d, 0)
    build_pick(8, 12)
    for d in (1, -1):
        side1[d].wait_recv()
        share(-d, 1)
    for d in (1, -1):
        near2[d].wait_recv()
        start(side4[d])
        start(side3[d])
        share(-2 * d, 1)
    a_hop(2, 0)
    far4[1].wait_recv()
    far4[-1].wait_recv()
    share(FAR, 0)
    for d in (1, -1):
        far3[d].wait_recv()
        share(-3 * d, 0)
    build_pick(12, 16)
    a_hop(1, 1)
    for d in (1, -1):
        side3[d].wait_recv()
        share(-3 * d, 1)
    side4[1].wait_recv()
    side4[-1].wait_recv()
    share(FAR, 1)
    a_hop(3, 0)
    own_g.wait()
    own_w.wait()
    for key in shared:
        shared[key].wait_recv()

    def sums(first, last):
        rows = slice(first * rows_a, last * rows_a)
        aligned[rows, :] = jnp.dot(pick[rows, :], cot_all[...], preferred_element_type=F32).astype(BF16)
        partial[rows, :] = dot_nt(aligned[rows, :], w_vmem[...])

    def part_a(distance, h):
        i = z_place(distance, h)
        return partial[i * rows_a:(i + 1) * rows_a, :SPLIT]

    def part_b(distance, h):
        i = z_place(distance, h)
        return partial[i * rows_a:(i + 1) * rows_a, SPLIT:]

    def encode(value, out, scale):
        top = jnp.maximum(jnp.max(jnp.abs(value), axis=0, keepdims=True), 1e-34)
        out[...] = jnp.round(value * (32767.0 / top)).astype(jnp.int32).astype(I16)
        scale[...] = top * (1.0 / 32767.0)

    def decode(data, scale):
        return data[...].astype(jnp.int32).astype(F32) * scale[...]

    class Parcel:
        def __init__(self, refs, sems, slot, device, rows=None):
            out, out_s, got, got_s = (ref.at[slot] for ref in refs)
            if rows is not None:
                out, got = out.at[pl.ds(0, rows)], got.at[pl.ds(0, rows)]
            self.out, self.out_s, self.got, self.got_s = out, out_s, got, got_s
            self.data = remote(out, got, sems.at[0, slot], sems.at[1, slot], device)
            self.scale = remote(out_s, got_s, sems.at[2, slot], sems.at[3, slot], device)

        def post(self, value):
            encode(value, self.out, self.out_s)
            start(self.data)
            start(self.scale)

        def fetch(self):
            self.data.wait_recv()
            self.scale.wait_recv()
            return decode(self.got, self.got_s)

    za_refs = (za_out, za_out_s, za_in, za_in_s)
    za = {}
    for level in range(FAR, 0, -1):
        for d, h in STREAMS:
            if level <= hops(d, h):
                za[(level, d, h)] = Parcel(za_refs, za_sem, len(za), at_z(d))
    xa = Parcel(za_refs, za_sem, len(za), x_far)
    xb = {g: Parcel((xb_out, xb_out_s, xb_in, xb_in_s), xb_sem, i, x_far) for i, g in enumerate(DISTANCES)}
    zb = {}
    for level in range(FAR, 0, -1):
        for d in (1, -1):
            rows = rows_h if level == FAR else None
            zb[(level, d)] = Parcel((zb_out, zb_out_s, zb_in, zb_in_s), zb_sem, len(zb), at_z(2 * d if level == FAR else d), rows)

    def a_first(level, d, h):
        za[(level, d, h)].post(part_a(level * d, h))

    def a_next(level, d, h):
        za[(level, d, h)].post(za[(level + 1, d, h)].fetch() + part_a(level * d, h))

    def b_cross(distance):
        xb[distance].post(part_b(distance, 1))

    def b_first():
        value = part_b(FAR, 0) + xb[FAR].fetch()
        zb[(FAR, 1)].post(value[:rows_h])
        zb[(FAR, -1)].post(value[rows_h:])

    def b_next(level, d):
        value = part_b(level * d, 0) + xb[level * d].fetch()
        if level < 3:
            value = value + zb[(level + 1, d)].fetch()
        if level == 2:
            got = zb[(FAR, d)].fetch()
            if d == 1:
                value = jnp.concatenate([value[:rows_h] + got, value[rows_h:]], axis=0)
            else:
                value = jnp.concatenate([value[:rows_h], value[rows_h:] + got], axis=0)
        zb[(level, d)].post(value)

    def wgrad_tiles(first, last):
        def tile(t, carry):
            at = pl.ds(pl.multiple_of(t * 128, 128), 128)
            wgrad[at, :] = dot_tn(act_all[:, at], aligned[...]).astype(BF16)
            return carry

        lax.fori_loop(first, last, tile, 0)

    sums(0, 2)
    b_cross(4)
    a_first(4, -1, 1)
    a_first(4, 1, 0)
    sums(2, 6)
    b_cross(3)
    b_cross(-3)
    a_first(3, 1, 1)
    a_first(3, -1, 0)
    a_hop(2, 1)
    sums(6, 10)
    b_cross(2)
    b_cross(-2)
    b_first()
    a_next(3, -1, 1)
    a_next(3, 1, 0)
    sums(10, 16)
    b_next(3, 1)
    b_next(3, -1)
    b_cross(1)
    b_cross(-1)
    a_next(2, 1, 1)
    a_next(2, -1, 0)
    a_next(2, -1, 1)
    a_next(2, 1, 0)
    a_hop(3, 1)
    b_next(2, 1)
    b_next(2, -1)
    b_cross(0)
    a_next(1, 1, 1)
    a_next(1, -1, 0)
    a_next(1, -1, 1)
    a_next(1, 1, 0)
    b_next(1, 1)
    b_next(1, -1)
    a_hop(4, 0)
    a_hop(4, 1)
    own_a.wait()
    xa.post(part_a(0, 1) + za[(1, 1, 1)].fetch() + za[(1, -1, 1)].fetch())
    wgrad_tiles(0, 7)
    home_a = part_a(0, 0) + za[(1, -1, 0)].fetch() + za[(1, 1, 0)].fetch() + xa.fetch()
    igrad[:, :SPLIT] = home_a.astype(BF16)
    home_b = part_b(0, 0) + xb[0].fetch() + zb[(1, 1)].fetch() + zb[(1, -1)].fetch()
    igrad[:, SPLIT:] = home_b.astype(BF16)
    for copy in sent:
        copy.wait_send()


def body(activations, cotangent, down_weight, row_order):
    rows_a, hidden = activations.shape
    rows_g, width = cotangent.shape
    total = row_order.shape[0]
    hbm = pl.BlockSpec(memory_space=pltpu.HBM)
    dma = pltpu.SemaphoreType.DMA

    def parcels(slots, columns):
        return [
            pltpu.VMEM((slots, rows_a, columns), I16),
            pltpu.VMEM((slots, 1, columns), F32),
            pltpu.VMEM((slots, rows_a, columns), I16),
            pltpu.VMEM((slots, 1, columns), F32),
        ]

    operands = (activations, cotangent, down_weight, row_order.reshape(total // 128, 128))
    return pl.pallas_call(
        kernel,
        out_shape=(
            jax.ShapeDtypeStruct((hidden, width), BF16),
            jax.ShapeDtypeStruct((rows_a, hidden), BF16),
        ),
        in_specs=[hbm] * 4,
        out_specs=(pl.BlockSpec(memory_space=pltpu.VMEM),) * 2,
        scratch_shapes=[
            pltpu.VMEM((total, width), BF16),
            pltpu.VMEM((total, hidden), BF16),
            pltpu.VMEM((hidden, width), BF16),
            pltpu.VMEM((total // 128, 128), jnp.int32),
            pltpu.VMEM((total, 128), F32),
            pltpu.VMEM((total, total), BF16),
            pltpu.VMEM((total, width), BF16),
            pltpu.VMEM((total, hidden), F32),
            *parcels(15, SPLIT),
            *parcels(8, hidden - SPLIT),
            *parcels(8, hidden - SPLIT),
            dma((17,)), dma((17,)), dma((16,)), dma((16,)), dma((15,)), dma((15,)),
            dma((4, 15)), dma((4, 8)), dma((4, 8)), dma((4,)),
        ],
        compiler_params=pltpu.CompilerParams(
            collective_id=0, has_side_effects=True, vmem_limit_bytes=40 * 1024 * 1024
        ),
    )(*(pltpu.with_memory_space_constraint(x, pltpu.HBM) for x in operands))


def solution(mesh):
    in_specs = (P("row", "col"), P("col", "row"), P("col", "row"), P())
    out_specs = (P("col", "row"), P("row", "col"))
    return jax.shard_map(body, mesh=mesh, in_specs=in_specs, out_specs=out_specs, check_vma=False)
```
